32 devices in a mesh: wide: 16 (over z, y, x), narrow: 2 (over core).
Axes of the slice: x: 2, y: 2, z: 4, core: 2. Of those that a mesh axis runs over, the one named last changes fastest.
Arguments:
- t_amps: bfloat16 [512, 32768], P('wide', 'narrow'), may hold values from -6 to 6
- v_blocks: bfloat16 [2, 16, 64, 128, 128], P('narrow', 'wide'), may hold values from -0.25 to 0.25
- block_pos: int32 [2, 16, 64], P('narrow', 'wide'), may hold values from 0 to 2047, as said below
- block_count: int32 [2, 16], P('narrow', 'wide'), may hold values from 24 to 64, as said below
Outputs:
- ladder: float32 [512, 32768], P('narrow', 'wide')
The draws below stay inside these ranges and needn't reach their ends.
Inputs may be any that keep to these rules, and one draw needn't show every extreme that they name: `block_pos`: within one tile the places of all 64 slots are distinct, and they lie in at most 64 distinct block rows. `block_count`: some tile holds exactly 64 stored blocks; loads are skewed, most tiles holding far fewer.
All inputs are finite; a program needn't handle non-finite values.
Results may differ from the reference program's by a relative error of at most 0.0003.
Values may be sent and summed in bfloat16 or wider, within the bound.
A program may use at most 320 MiB of HBM per device.

```python
import jax
import jax.numpy as jnp
from jax import lax

OP = 512
W = 32768
BS = 128
MAXB = 64
RB = 128
CB = 16
N_WIDE = 16
N_NARROW = 2


def draw_block_pos(key, part):
    half_rows = RB // 2
    keys = jax.random.split(jax.random.fold_in(key, 11), N_NARROW * N_WIDE)

    def one_tile(tile_key):
        row_key, place_key = jax.random.split(tile_key)
        row_scores = jax.random.randint(row_key, (RB,), 0, (1 << 30) // RB) * RB
        row_scores = row_scores + jnp.arange(RB, dtype=jnp.int32)
        chosen_rows = jnp.argsort(row_scores, stable=True)[:half_rows].astype(jnp.int32)
        total = half_rows * CB
        scores = jax.random.randint(place_key, (total,), 0, (1 << 30) // total) * total
        scores = scores + jnp.arange(total, dtype=jnp.int32)
        picked = jnp.argsort(scores, stable=True)[:MAXB].astype(jnp.int32)
        return chosen_rows[picked // CB] * CB + picked % CB
    places = jax.vmap(one_tile)(keys)
    return places.astype(jnp.int32).reshape(N_NARROW, N_WIDE, MAXB)


def draw_block_count(key, part):
    lowest = MAXB * 3 // 8
    draws = jax.random.randint(jax.random.fold_in(key, 23), (N_NARROW * N_WIDE,), 0, 1000)
    counts = lowest + draws * draws * (MAXB - lowest) // 998001
    fullest = jax.random.randint(jax.random.fold_in(key, 37), (), 0, N_NARROW * N_WIDE)
    counts = counts.at[fullest].set(MAXB)
    return counts.astype(jnp.int32).reshape(N_NARROW, N_WIDE)


def level_of(stream_key, shape, pieces, low, largest):
    level = 1.0
    for axis_at, parts in pieces:
        steps = jax.random.uniform(jax.random.fold_in(jax.random.fold_in(stream_key, 6), axis_at), (parts,), jnp.float32, low / len(pieces), largest / len(pieces))
        level = level * jnp.repeat(jnp.exp(steps), shape[axis_at] // parts).reshape((-1,) + (1,) * (len(shape) - 1 - axis_at))
    return level


def gaussian(key, dims, scale, most, pieces=(), kind=jnp.bfloat16):
    entries = jax.random.normal(key, dims, jnp.float32) * scale
    if len(pieces) > 0:
        entries = level_of(key, dims, pieces, -0.22, 0.18) * entries
    return jnp.clip(entries, min=-most, max=most).astype(kind)


def setup_inputs(seed: int = 0) -> dict:
    streams_of = jax.random.split(jax.random.key(seed), 5)
    t_amps = gaussian(streams_of[0], (OP, W), 1.0, 6.0, ((0, 16), (1, 2)))
    v_blocks = gaussian(streams_of[1], (N_NARROW, N_WIDE, MAXB, BS, BS), (MAXB * N_NARROW * BS // (2 * CB)) ** -0.5, 0.25, ((0, 2), (1, 16)))
    block_pos = draw_block_pos(jax.random.fold_in(streams_of[4], 71), 0)
    block_count = draw_block_count(jax.random.fold_in(streams_of[4], 71), 0)
    return dict(t_amps=t_amps, v_blocks=v_blocks, block_pos=block_pos, block_count=block_count)


def reference(t_amps, v_blocks, block_pos, block_count):
    slots = jnp.arange(MAXB, dtype=jnp.int32)
    col_ids = jnp.arange(CB, dtype=jnp.int32)

    def strip(w_index):
        def over_slice(accum, n_index):
            start = (n_index * (RB * BS)).astype(jnp.int32)
            t_part = lax.dynamic_slice_in_dim(t_amps, start, RB * BS, 1).astype(jnp.float32)
            t_part = t_part.reshape(OP, RB, BS)
            places = block_pos[n_index, w_index]
            row_index = places // CB
            col_index = places % CB
            live_mask = (slots < block_count[n_index, w_index]).astype(jnp.float32)
            stored = v_blocks[n_index, w_index].astype(jnp.float32) * live_mask[:, None, None]
            chosen = jnp.take(t_part, row_index, axis=1)
            products = jnp.einsum("ogk,gkm->ogm", chosen, stored, precision=lax.Precision.HIGHEST)
            one_hot = (col_index[:, None] == col_ids[None, :]).astype(jnp.float32)
            return accum + jnp.einsum("ogm,gc->ocm", products, one_hot, precision=lax.Precision.HIGHEST), None

        start_acc = jnp.zeros((OP, CB, BS), jnp.float32)
        accum, unused = lax.scan(over_slice, start_acc, jnp.arange(N_NARROW, dtype=jnp.int32))
        return accum.reshape(OP, CB * BS)

    strips = lax.map(strip, jnp.arange(N_WIDE, dtype=jnp.int32))
    return jnp.transpose(strips, (1, 0, 2)).reshape(OP, W)
```

```python
import functools

import jax
import jax.numpy as jnp
from jax import lax
from jax.experimental import pallas as pl
from jax.experimental.pallas import tpu as pltpu
from jax.sharding import PartitionSpec as P

MESH = pl.DeviceIdType.MESH


def dense_shards(width, t_amps, v_blocks, block_pos, block_count):
    stored = v_blocks[0, 0]
    places = block_pos[0, 0]
    slot_count = block_count[0, 0]
    block_size = stored.shape[1]
    slot_total = stored.shape[0]
    row_blocks = t_amps.shape[1] // block_size
    col_blocks = width // (lax.axis_size("wide") * block_size)
    live_mask = (jnp.arange(slot_total, dtype=jnp.int32) < slot_count).astype(jnp.bfloat16)
    masked = stored * live_mask[:, None, None]
    dense_tile = jnp.zeros((row_blocks * col_blocks, block_size, block_size), jnp.bfloat16)
    dense_tile = dense_tile.at[places].add(masked)
    dense_tile = dense_tile.reshape(row_blocks, col_blocks, block_size, block_size)
    dense_tile = jnp.transpose(dense_tile, (0, 2, 1, 3)).reshape(row_blocks * block_size, col_blocks * block_size)
    gathered = lax.all_gather(t_amps, "wide", axis=0, tiled=True)
    partial_sum = jnp.dot(gathered, dense_tile, preferred_element_type=jnp.float32)
    return lax.psum_scatter(partial_sum, "narrow", scatter_dimension=0, tiled=True)


def ladder_kernel(depth, t, v_tile, meta_v, out, *scratch):
    bufs = scratch[: 2 * depth - 1]
    (v_own, v_other, meta_in, meta, meta_other, runs, part, core_in, y_out, local_sem, az_send, az_recv, bz_send, bz_recv,
     ax_send, ax_recv, one_send, one_recv, core_send, core_recv, y_send, y_recv) = scratch[2 * depth - 1:]
    wide, core = lax.axis_index("wide"), lax.axis_index("narrow")
    z, y, x = wide // 4, (wide // 2) % 2, wide % 2
    up, down = (wide + 4, core), (wide - 4, core)
    across = (wide + 1 - 2 * x, core)
    beside = (wide + 2 - 4 * y, core)
    twin = (wide, 1 - core)
    half = depth // 2
    row_blocks, rows, unused = t.shape
    v = v_tile.at[0, 0]
    slots, size = v.shape[0], v.shape[1]
    col_blocks = out.shape[-1] // size
    second = row_blocks * 5 // 32
    first = row_blocks - second
    first_cols, second_cols = pl.ds(0, first), pl.ds(first, second)
    has_up, has_down = z < depth - 1, z > 0

    def copy(src, dst, send, recv, device):
        return pltpu.make_async_remote_copy(
            src_ref=src, dst_ref=dst, send_sem=send, recv_sem=recv, device_id=device, device_id_type=MESH
        )

    def place(b):
        if b == 0:
            return z, None
        if b < depth:
            return z - b, z >= b
        return z + (b - depth + 1), z + (b - depth + 1) < depth

    def guarded(cond, fn):
        if cond is None:
            fn()
        else:
            pl.when(cond)(fn)

    def both(a, b):
        return b if a is None else a if b is None else jnp.logical_and(a, b)

    def from_own(cols):
        return t.at[cols]

    def hops(b):
        moves = []
        if b < depth - 1:
            moves.append((b + 1, up, has_up, b))
        if b == 0 or depth <= b < 2 * depth - 2:
            landing = depth if b == 0 else b + 1
            moves.append((landing, down, has_down, depth - 1 + (landing - depth)))
        return moves

    def az(b, move):
        landing, device, unused, sem = move
        src = from_own(first_cols) if b == 0 else bufs[b].at[x, first_cols]
        return copy(src, bufs[landing].at[x, first_cols], az_send.at[sem], az_recv.at[landing], device)

    def bz(b, move):
        landing, device, unused, sem = move
        return copy(bufs[b].at[:, second_cols], bufs[landing].at[:, second_cols], bz_send.at[sem], bz_recv.at[landing], device)

    def ax(b):
        src = from_own(first_cols) if b == 0 else bufs[b].at[x, first_cols]
        return copy(src, bufs[b].at[x, first_cols], ax_send.at[b], ax_recv.at[b], across)

    def az_wait(b):
        dst = bufs[b].at[x, first_cols]
        copy(dst, dst, az_send.at[0], az_recv.at[b], up).wait_recv()

    def bz_wait(b):
        dst = bufs[b].at[:, second_cols]
        copy(dst, dst, bz_send.at[0], bz_recv.at[b], up).wait_recv()

    def ax_wait(b):
        dst = bufs[b].at[1 - x, first_cols]
        copy(dst, dst, ax_send.at[b], ax_recv.at[b], across).wait_recv()

    barrier = pltpu.get_barrier_semaphore()
    for device in (across, beside, twin):
        pl.semaphore_signal(barrier, inc=1, device_id=device, device_id_type=MESH)
    pl.when(has_up)(lambda: pl.semaphore_signal(barrier, inc=1, device_id=up, device_id_type=MESH))
    pl.when(has_down)(lambda: pl.semaphore_signal(barrier, inc=1, device_id=down, device_id_type=MESH))
    pl.semaphore_wait(barrier, 3 + has_up.astype(jnp.int32) + has_down.astype(jnp.int32))

    bx = copy(from_own(second_cols), bufs[0].at[x, second_cols], one_send.at[0], one_recv.at[0], across)
    vy = copy(v, v_other, one_send.at[1], one_recv.at[1], beside)
    my = copy(meta_v, meta_in, one_send.at[2], one_recv.at[2], beside)
    bx.start()
    for move in hops(0):
        guarded(move[2], lambda move=move: az(0, move).start())
    ax(0).start()
    my.start()
    vy.start()
    own_t = pltpu.make_async_copy(t, bufs[0].at[x], local_sem.at[0])
    own_v = pltpu.make_async_copy(v, v_own, local_sem.at[1])
    own_t.start()
    own_v.start()
    own_m = pltpu.make_async_copy(meta_v, meta, local_sem.at[3])
    own_m.start()
    own_m.wait()
    own_t.wait()
    bx.wait_recv()
    for move in hops(0):
        guarded(move[2], lambda move=move: bz(0, move).start())

    def forward(b):
        def run():
            az_wait(b)
            for move in hops(b):
                guarded(move[2], lambda move=move: az(b, move).start())
            ax(b).start()
            bz_wait(b)
            for move in hops(b):
                guarded(move[2], lambda move=move: bz(b, move).start())

        guarded(place(b)[1], run)

    def products(b, strip, stored, info):
        zp = place(b)[0]

        def slot(s, carry):
            at_row = info[1, s]
            left = jnp.concatenate([bufs[b][0, at_row], bufs[b][1, at_row]], axis=0)
            new = jnp.dot(left, stored[info[0, s]], preferred_element_type=jnp.float32)
            runs[s + 1] = new + runs[s] * info[2, s].astype(jnp.float32)
            return carry

        runs[0] = jnp.zeros((2 * rows, size), jnp.float32)
        lax.fori_loop(0, slots, slot, 0, unroll=8)
        for c in range(col_blocks):
            value = runs[info[3, c] + 1] * info[4, c].astype(jnp.float32)
            part[zp, strip, :, c * size:(c + 1) * size] = value

    def core_copy(b, strip):
        zp = place(b)[0]
        return copy(part.at[zp, strip], core_in.at[zp % half, strip], core_send.at[b, strip], core_recv.at[b, strip], twin)

    def out_rows(b):
        return pl.ds(pl.multiple_of((place(b)[0] % half * 2 + y) * 2 * rows, 2 * rows), 2 * rows)

    def y_copy(b):
        return copy(y_out.at[place(b)[0] % half], out.at[out_rows(b), :], y_send.at[b], y_recv.at[b], beside)

    def mine(b):
        return place(b)[0] // half == core

    def compute(b):
        def run():
            ax_wait(b)
            for strip, stored, info in ((0, v_other, meta_other), (1, v_own, meta)):
                products(b, strip, stored, info)
                pl.when(jnp.logical_not(mine(b)))(lambda strip=strip: core_copy(b, strip).start())

        guarded(place(b)[1], run)

    def finish(b):
        def run():
            zp = place(b)[0]
            slot = zp % half
            core_copy(b, 0).wait_recv()
            y_out[slot] = part[zp, 0] + core_in[slot, 0]
            y_copy(b).start()
            core_copy(b, 1).wait_recv()
            out[out_rows(b), :] = part[zp, 1] + core_in[slot, 1]

        guarded(both(place(b)[1], mine(b)), run)

    def at(k):
        return [0] if k == 0 else [k, depth - 1 + k]

    ready = done = 0
    for k in range(1, depth):
        for b in at(k):
            forward(b)
        if k == min(2, depth - 1):
            own_v.wait()
            my.wait_recv()
            into = pltpu.make_async_copy(meta_in, meta_other, local_sem.at[2])
            into.start()
            into.wait()
            vy.wait_recv()
        if k >= 2:
            while ready < (depth - 1 if k == depth - 1 else k - 1):
                for b in at(ready):
                    compute(b)
                ready += 1
                if ready - 2 >= done:
                    for b in at(done):
                        finish(b)
                    done += 1
    while ready < depth:
        for b in at(ready):
            compute(b)
        ready += 1
    while done < depth:
        for b in at(done):
            finish(b)
        done += 1

    bx.wait_send()
    vy.wait_send()
    my.wait_send()
    for b in range(2 * depth - 1):
        valid = place(b)[1]
        for move in hops(b):
            guarded(both(valid, move[2]), lambda b=b, move=move: (az(b, move).wait_send(), bz(b, move).wait_send(), None)[-1])
        guarded(valid, lambda b=b: ax(b).wait_send())
        other = jnp.logical_not(mine(b))
        guarded(both(valid, other), lambda b=b: (core_copy(b, 0).wait_send(), core_copy(b, 1).wait_send(), None)[-1])
        guarded(both(valid, mine(b)), lambda b=b: y_copy(b).wait())


def slot_table(places, count, col_blocks):
    total = places.shape[0]
    ids = jnp.arange(total, dtype=jnp.int32)
    cols = jnp.where(ids < count, places % col_blocks, col_blocks)
    key = cols * total + ids
    rank = jnp.sum((key[None, :] < key[:, None]).astype(jnp.int32), axis=1)
    hit = (rank[:, None] == ids[None, :]).astype(jnp.int32)
    order = jnp.sum(hit * ids[:, None], axis=0)
    row = jnp.sum(hit * (places // col_blocks)[:, None], axis=0)
    col = jnp.sum(hit * cols[:, None], axis=0)
    before = jnp.sum((rank[:, None] + 1 == ids[None, :]).astype(jnp.int32) * (cols + 1)[:, None], axis=0) - 1
    same = (col == before).astype(jnp.int32)
    each = jnp.arange(col_blocks, dtype=jnp.int32)
    last = jnp.sum((cols[None, :] <= each[:, None]).astype(jnp.int32), axis=1) - 1
    some = jnp.sum((cols[None, :] == each[:, None]).astype(jnp.int32), axis=1)
    lanes = -(-max(total, col_blocks) // 128) * 128

    def wide(a):
        return jnp.pad(a, (0, lanes - a.shape[0]))

    zero = jnp.zeros((lanes,), jnp.int32)
    return jnp.stack([wide(order), wide(row), wide(same), wide(jnp.maximum(last, 0)), wide(jnp.minimum(some, 1)), zero, zero, zero])


def ring_shards(width, wide_size, t_amps, v_blocks, block_pos, block_count):
    rows, columns = t_amps.shape
    slots, size = v_blocks.shape[2], v_blocks.shape[3]
    depth = wide_size // 4
    half, buffers = depth // 2, 2 * depth - 1
    strip = width // wide_size
    meta = slot_table(block_pos[0, 0], block_count[0, 0], strip // size)
    by_block = jnp.transpose(t_amps.reshape(rows, columns // size, size), (1, 0, 2))
    bf16, f32, i32 = jnp.bfloat16, jnp.float32, jnp.int32
    dma = pltpu.SemaphoreType.DMA
    out = pl.pallas_call(
        functools.partial(ladder_kernel, depth),
        out_shape=jax.ShapeDtypeStruct((half * 4 * rows, strip), f32),
        in_specs=[
            pl.BlockSpec(memory_space=pl.ANY),
            pl.BlockSpec(memory_space=pl.ANY),
            pl.BlockSpec(memory_space=pltpu.VMEM),
        ],
        out_specs=pl.BlockSpec(memory_space=pltpu.VMEM),
        scratch_shapes=[pltpu.VMEM((2, columns // size, rows, size), bf16)] * buffers + [
            pltpu.VMEM((slots, size, size), bf16),
            pltpu.VMEM((slots, size, size), bf16),
            pltpu.VMEM(meta.shape, i32),
            pltpu.SMEM(meta.shape, i32),
            pltpu.SMEM(meta.shape, i32),
            pltpu.VMEM((slots + 1, 2 * rows, size), f32),
            pltpu.VMEM((depth, 2, 2 * rows, strip), f32),
            pltpu.VMEM((half, 2, 2 * rows, strip), f32),
            pltpu.VMEM((half, 2 * rows, strip), f32),
            dma((4,)),
            dma((2 * depth,)), dma((buffers,)),
            dma((2 * depth,)), dma((buffers,)),
            dma((buffers,)), dma((buffers,)),
            dma((3,)), dma((3,)),
            dma((buffers, 2)), dma((buffers, 2)),
            dma((buffers,)), dma((buffers,)),
        ],
        compiler_params=pltpu.CompilerParams(
            collective_id=0, has_side_effects=True, vmem_limit_bytes=56 * 1024 * 1024
        ),
    )(by_block, v_blocks, meta)
    return out


def solution(mesh):
    in_specs = (
        P("wide", "narrow"),
        P("narrow", "wide", None, None, None),
        P("narrow", "wide", None),
        P("narrow", "wide"),
    )
    out_specs = P("narrow", "wide")
    wide_size, narrow_size = mesh.shape["wide"], mesh.shape["narrow"]

    def program(t_amps, v_blocks, block_pos, block_count):
        width = t_amps.shape[1]
        if narrow_size == 2 and wide_size % 8 == 0:
            body = functools.partial(ring_shards, width, wide_size)
        else:
            body = functools.partial(dense_shards, width)
        run = jax.shard_map(body, mesh=mesh, in_specs=in_specs, out_specs=out_specs, check_vma=False)
        return run(t_amps, v_blocks, block_pos, block_count)

    return program
```

```python
import functools

import jax
import jax.numpy as jnp
from jax import lax
from jax.experimental import pallas as pl
from jax.experimental.pallas import tpu as pltpu
from jax.sharding import PartitionSpec as P

MESH = pl.DeviceIdType.MESH
PIECES = 2


def dense_shards(width, t_amps, v_blocks, block_pos, block_count):
    stored = v_blocks[0, 0]
    places = block_pos[0, 0]
    slot_count = block_count[0, 0]
    block_size = stored.shape[1]
    slot_total = stored.shape[0]
    row_blocks = t_amps.shape[1] // block_size
    col_blocks = width // (lax.axis_size("wide") * block_size)
    live_mask = (jnp.arange(slot_total, dtype=jnp.int32) < slot_count).astype(jnp.bfloat16)
    masked = stored * live_mask[:, None, None]
    dense_tile = jnp.zeros((row_blocks * col_blocks, block_size, block_size), jnp.bfloat16)
    dense_tile = dense_tile.at[places].add(masked)
    dense_tile = dense_tile.reshape(row_blocks, col_blocks, block_size, block_size)
    dense_tile = jnp.transpose(dense_tile, (0, 2, 1, 3)).reshape(row_blocks * block_size, col_blocks * block_size)
    gathered = lax.all_gather(t_amps, "wide", axis=0, tiled=True)
    partial_sum = jnp.dot(gathered, dense_tile, preferred_element_type=jnp.float32)
    return lax.psum_scatter(partial_sum, "narrow", scatter_dimension=0, tiled=True)


def ladder_kernel(depth, t, v_tile, meta_v, out, *scratch):
    bufs = scratch[: 2 * depth - 1]
    (v_own, v_other, meta_in, meta, meta_other, runs, part, core_in, y_out, local_sem, az_send, az_recv, bz_send, bz_recv,
     ax_send, ax_recv, one_send, one_recv, core_send, core_recv, y_send, y_recv) = scratch[2 * depth - 1:]
    wide, core = lax.axis_index("wide"), lax.axis_index("narrow")
    z, y, x = wide // 4, (wide // 2) % 2, wide % 2
    up, down = (wide + 4, core), (wide - 4, core)
    across = (wide + 1 - 2 * x, core)
    beside = (wide + 2 - 4 * y, core)
    twin = (wide, 1 - core)
    half = depth // 2
    row_blocks, rows, unused = t.shape
    v = v_tile.at[0, 0]
    slots, size = v.shape[0], v.shape[1]
    col_blocks = out.shape[-1] // size
    second = row_blocks * 5 // 32
    first = row_blocks - second
    cuts = [first * q // PIECES for q in range(PIECES + 1)]
    pieces = [pl.ds(cuts[q], cuts[q + 1] - cuts[q]) for q in range(PIECES)]
    second_cols = pl.ds(first, second)
    has_up, has_down = z < depth - 1, z > 0

    def copy(src, dst, send, recv, device):
        return pltpu.make_async_remote_copy(
            src_ref=src, dst_ref=dst, send_sem=send, recv_sem=recv, device_id=device, device_id_type=MESH
        )

    def place(b):
        if b == 0:
            return z, None
        if b < depth:
            return z - b, z >= b
        return z + (b - depth + 1), z + (b - depth + 1) < depth

    def guarded(cond, fn):
        if cond is None:
            fn()
        else:
            pl.when(cond)(fn)

    def both(a, b):
        return b if a is None else a if b is None else jnp.logical_and(a, b)

    def from_own(cols):
        return t.at[cols]

    def hops(b):
        moves = []
        if b < depth - 1:
            moves.append((b + 1, up, has_up, b))
        if b == 0 or depth <= b < 2 * depth - 2:
            landing = depth if b == 0 else b + 1
            moves.append((landing, down, has_down, depth - 1 + (landing - depth)))
        return moves

    def az(b, move, q):
        landing, device, unused, sem = move
        src = from_own(pieces[q]) if b == 0 else bufs[b].at[x, pieces[q]]
        return copy(src, bufs[landing].at[x, pieces[q]], az_send.at[sem, q], az_recv.at[landing, q], device)

    def bz(b, move):
        landing, device, unused, sem = move
        return copy(bufs[b].at[:, second_cols], bufs[landing].at[:, second_cols], bz_send.at[sem], bz_recv.at[landing], device)

    def ax(b, q):
        src = from_own(pieces[q]) if b == 0 else bufs[b].at[x, pieces[q]]
        return copy(src, bufs[b].at[x, pieces[q]], ax_send.at[b, q], ax_recv.at[b, q], across)

    def az_wait(b, q):
        dst = bufs[b].at[x, pieces[q]]
        copy(dst, dst, az_send.at[0, q], az_recv.at[b, q], up).wait_recv()

    def bz_wait(b):
        dst = bufs[b].at[:, second_cols]
        copy(dst, dst, bz_send.at[0], bz_recv.at[b], up).wait_recv()

    def ax_wait(b):
        for q in range(PIECES):
            dst = bufs[b].at[1 - x, pieces[q]]
            copy(dst, dst, ax_send.at[b, q], ax_recv.at[b, q], across).wait_recv()

    barrier = pltpu.get_barrier_semaphore()
    for device in (across, beside, twin):
        pl.semaphore_signal(barrier, inc=1, device_id=device, device_id_type=MESH)
    pl.when(has_up)(lambda: pl.semaphore_signal(barrier, inc=1, device_id=up, device_id_type=MESH))
    pl.when(has_down)(lambda: pl.semaphore_signal(barrier, inc=1, device_id=down, device_id_type=MESH))
    pl.semaphore_wait(barrier, 3 + has_up.astype(jnp.int32) + has_down.astype(jnp.int32))

    bx = copy(from_own(second_cols), bufs[0].at[x, second_cols], one_send.at[0], one_recv.at[0], across)
    vy = copy(v, v_other, one_send.at[1], one_recv.at[1], beside)
    my = copy(meta_v, meta_in, one_send.at[2], one_recv.at[2], beside)
    bx.start()
    for q in range(PIECES):
        for move in hops(0):
            guarded(move[2], lambda move=move, q=q: az(0, move, q).start())
        ax(0, q).start()
    my.start()
    vy.start()
    own_t = pltpu.make_async_copy(t, bufs[0].at[x], local_sem.at[0])
    own_v = pltpu.make_async_copy(v, v_own, local_sem.at[1])
    own_t.start()
    own_v.start()
    own_m = pltpu.make_async_copy(meta_v, meta, local_sem.at[3])
    own_m.start()
    own_m.wait()
    own_t.wait()
    bx.wait_recv()

    def second_own(k):
        for move, turn in zip(hops(0), (z, depth - 1 - z)):
            guarded(both(move[2], turn == k), lambda move=move: bz(0, move).start())

    def forward(b, q):
        def run():
            az_wait(b, q)
            for move in hops(b):
                guarded(move[2], lambda move=move: az(b, move, q).start())
            ax(b, q).start()

        guarded(place(b)[1], run)

    def forward_second(b):
        def run():
            bz_wait(b)
            for move in hops(b):
                guarded(move[2], lambda move=move: bz(b, move).start())

        guarded(place(b)[1], run)

    def products(b, strip, stored, info):
        zp = place(b)[0]

        def slot(s, carry):
            at_row = info[1, s]
            left = jnp.concatenate([bufs[b][0, at_row], bufs[b][1, at_row]], axis=0)
            new = jnp.dot(left, stored[info[0, s]], preferred_element_type=jnp.float32)
            runs[s + 1] = new + runs[s] * info[2, s].astype(jnp.float32)
            return carry

        runs[0] = jnp.zeros((2 * rows, size), jnp.float32)
        lax.fori_loop(0, slots, slot, 0, unroll=8)
        for c in range(col_blocks):
            value = runs[info[3, c] + 1] * info[4, c].astype(jnp.float32)
            part[zp, strip, :, c * size:(c + 1) * size] = value

    def core_copy(b, strip):
        zp = place(b)[0]
        return copy(part.at[zp, strip], core_in.at[zp % half, strip], core_send.at[b, strip], core_recv.at[b, strip], twin)

    def out_rows(b):
        return pl.ds(pl.multiple_of((place(b)[0] % half * 2 + y) * 2 * rows, 2 * rows), 2 * rows)

    def y_copy(b):
        return copy(y_out.at[place(b)[0] % half], out.at[out_rows(b), :], y_send.at[b], y_recv.at[b], beside)

    def mine(b):
        return place(b)[0] // half == core

    def compute(b):
        def run():
            ax_wait(b)
            for strip, stored, info in ((0, v_other, meta_other), (1, v_own, meta)):
                products(b, strip, stored, info)
                pl.when(jnp.logical_not(mine(b)))(lambda strip=strip: core_copy(b, strip).start())

        guarded(place(b)[1], run)

    def finish(b):
        def run():
            zp = place(b)[0]
            slot = zp % half
            core_copy(b, 0).wait_recv()
            y_out[slot] = part[zp, 0] + core_in[slot, 0]
            y_copy(b).start()
            core_copy(b, 1).wait_recv()
            out[out_rows(b), :] = part[zp, 1] + core_in[slot, 1]

        guarded(both(place(b)[1], mine(b)), run)

    def at(k):
        return [0] if k == 0 else [k, depth - 1 + k]

    second_own(0)
    for k in range(1, depth):
        for q in range(PIECES):
            for b in at(k):
                forward(b, q)
        second_own(k)
    own_v.wait()
    my.wait_recv()
    into = pltpu.make_async_copy(meta_in, meta_other, local_sem.at[2])
    into.start()
    into.wait()
    vy.wait_recv()
    compute(0)
    for k in range(1, depth):
        for b in at(k):
            forward_second(b)
        for b in at(k - 1):
            finish(b)
        for b in at(k):
            compute(b)
    for b in at(depth - 1):
        finish(b)

    bx.wait_send()
    vy.wait_send()
    my.wait_send()
    for b in range(2 * depth - 1):
        valid = place(b)[1]
        for move in hops(b):
            guarded(both(valid, move[2]), lambda b=b, move=move: [az(b, move, q).wait_send() for q in range(PIECES)] and bz(b, move).wait_send())
        guarded(valid, lambda b=b: [ax(b, q).wait_send() for q in range(PIECES)] and None)
        other = jnp.logical_not(mine(b))
        guarded(both(valid, other), lambda b=b: (core_copy(b, 0).wait_send(), core_copy(b, 1).wait_send(), None)[-1])
        guarded(both(valid, mine(b)), lambda b=b: y_copy(b).wait())


def slot_table(places, count, col_blocks):
    total = places.shape[0]
    ids = jnp.arange(total, dtype=jnp.int32)
    cols = jnp.where(ids < count, places % col_blocks, col_blocks)
    key = cols * total + ids
    rank = jnp.sum((key[None, :] < key[:, None]).astype(jnp.int32), axis=1)
    hit = (rank[:, None] == ids[None, :]).astype(jnp.int32)
    order = jnp.sum(hit * ids[:, None], axis=0)
    row = jnp.sum(hit * (places // col_blocks)[:, None], axis=0)
    col = jnp.sum(hit * cols[:, None], axis=0)
    before = jnp.sum((rank[:, None] + 1 == ids[None, :]).astype(jnp.int32) * (cols + 1)[:, None], axis=0) - 1
    same = (col == before).astype(jnp.int32)
    each = jnp.arange(col_blocks, dtype=jnp.int32)
    last = jnp.sum((cols[None, :] <= each[:, None]).astype(jnp.int32), axis=1) - 1
    some = jnp.sum((cols[None, :] == each[:, None]).astype(jnp.int32), axis=1)
    lanes = -(-max(total, col_blocks) // 128) * 128

    def wide(a):
        return jnp.pad(a, (0, lanes - a.shape[0]))

    zero = jnp.zeros((lanes,), jnp.int32)
    return jnp.stack([wide(order), wide(row), wide(same), wide(jnp.maximum(last, 0)), wide(jnp.minimum(some, 1)), zero, zero, zero])


def ring_shards(width, wide_size, t_amps, v_blocks, block_pos, block_count):
    rows, columns = t_amps.shape
    slots, size = v_blocks.shape[2], v_blocks.shape[3]
    depth = wide_size // 4
    half, buffers = depth // 2, 2 * depth - 1
    strip = width // wide_size
    meta = slot_table(block_pos[0, 0], block_count[0, 0], strip // size)
    by_block = jnp.transpose(t_amps.reshape(rows, columns // size, size), (1, 0, 2))
    bf16, f32, i32 = jnp.bfloat16, jnp.float32, jnp.int32
    dma = pltpu.SemaphoreType.DMA
    out = pl.pallas_call(
        functools.partial(ladder_kernel, depth),
        out_shape=jax.ShapeDtypeStruct((half * 4 * rows, strip), f32),
        in_specs=[
            pl.BlockSpec(memory_space=pl.ANY),
            pl.BlockSpec(memory_space=pl.ANY),
            pl.BlockSpec(memory_space=pltpu.VMEM),
        ],
        out_specs=pl.BlockSpec(memory_space=pltpu.VMEM),
        scratch_shapes=[pltpu.VMEM((2, columns // size, rows, size), bf16)] * buffers + [
            pltpu.VMEM((slots, size, size), bf16),
            pltpu.VMEM((slots, size, size), bf16),
            pltpu.VMEM(meta.shape, i32),
            pltpu.SMEM(meta.shape, i32),
            pltpu.SMEM(meta.shape, i32),
            pltpu.VMEM((slots + 1, 2 * rows, size), f32),
            pltpu.VMEM((depth, 2, 2 * rows, strip), f32),
            pltpu.VMEM((half, 2, 2 * rows, strip), f32),
            pltpu.VMEM((half, 2 * rows, strip), f32),
            dma((4,)),
            dma((2 * depth, PIECES)), dma((buffers, PIECES)),
            dma((2 * depth,)), dma((buffers,)),
            dma((buffers, PIECES)), dma((buffers, PIECES)),
            dma((3,)), dma((3,)),
            dma((buffers, 2)), dma((buffers, 2)),
            dma((buffers,)), dma((buffers,)),
        ],
        compiler_params=pltpu.CompilerParams(
            collective_id=0, has_side_effects=True, vmem_limit_bytes=56 * 1024 * 1024
        ),
    )(by_block, v_blocks, meta)
    return out


def solution(mesh):
    in_specs = (
        P("wide", "narrow"),
        P("narrow", "wide", None, None, None),
        P("narrow", "wide", None),
        P("narrow", "wide"),
    )
    out_specs = P("narrow", "wide")
    wide_size, narrow_size = mesh.shape["wide"], mesh.shape["narrow"]

    def program(t_amps, v_blocks, block_pos, block_count):
        width = t_amps.shape[1]
        if narrow_size == 2 and wide_size % 8 == 0:
            body = functools.partial(ring_shards, width, wide_size)
        else:
            body = functools.partial(dense_shards, width)
        run = jax.shard_map(body, mesh=mesh, in_specs=in_specs, out_specs=out_specs, check_vma=False)
        return run(t_amps, v_blocks, block_pos, block_count)

    return program
```

```python
import functools

import jax
import jax.numpy as jnp
from jax import lax
from jax.experimental import pallas as pl
from jax.experimental.pallas import tpu as pltpu
from jax.sharding import PartitionSpec as P

MESH = pl.DeviceIdType.MESH
PIECES = 2


def dense_shards(width, t_amps, v_blocks, block_pos, block_count):
    stored = v_blocks[0, 0]
    places = block_pos[0, 0]
    slot_count = block_count[0, 0]
    block_size = stored.shape[1]
    slot_total = stored.shape[0]
    row_blocks = t_amps.shape[1] // block_size
    col_blocks = width // (lax.axis_size("wide") * block_size)
    live_mask = (jnp.arange(slot_total, dtype=jnp.int32) < slot_count).astype(jnp.bfloat16)
    masked = stored * live_mask[:, None, None]
    dense_tile = jnp.zeros((row_blocks * col_blocks, block_size, block_size), jnp.bfloat16)
    dense_tile = dense_tile.at[places].add(masked)
    dense_tile = dense_tile.reshape(row_blocks, col_blocks, block_size, block_size)
    dense_tile = jnp.transpose(dense_tile, (0, 2, 1, 3)).reshape(row_blocks * block_size, col_blocks * block_size)
    gathered = lax.all_gather(t_amps, "wide", axis=0, tiled=True)
    partial_sum = jnp.dot(gathered, dense_tile, preferred_element_type=jnp.float32)
    return lax.psum_scatter(partial_sum, "narrow", scatter_dimension=0, tiled=True)


def ladder_kernel(depth, t, v_tile, meta_v, out, *scratch):
    held = scratch[: (2 * depth - 1) * PIECES]
    bufs = [held[b * PIECES:(b + 1) * PIECES] for b in range(2 * depth - 1)]
    (v_own, v_other, meta_in, meta, meta_other, runs, part, core_in, y_out, own_out, own_sem, lay_sem, bx_send, bx_recv, local_sem, az_send, az_recv, bz_send, bz_recv,
     ax_send, ax_recv, one_send, one_recv, core_send, core_recv, y_send, y_recv) = scratch[(2 * depth - 1) * PIECES:]
    wide, core = lax.axis_index("wide"), lax.axis_index("narrow")
    z, y, x = wide // 4, (wide // 2) % 2, wide % 2
    up, down = (wide + 4, core), (wide - 4, core)
    across = (wide + 1 - 2 * x, core)
    beside = (wide + 2 - 4 * y, core)
    twin = (wide, 1 - core)
    half = depth // 2
    rows, columns = t.shape
    v = v_tile.at[0, 0]
    slots, size = v.shape[0], v.shape[1]
    row_blocks = columns // size
    col_blocks = out.shape[-1] // size
    second = row_blocks * 4 // 32
    first = row_blocks - second
    chunk = rows // PIECES
    first_cols = pl.ds(0, first)
    second_cols = pl.ds(first, second)
    has_up, has_down = z < depth - 1, z > 0

    def copy(src, dst, send, recv, device):
        return pltpu.make_async_remote_copy(
            src_ref=src, dst_ref=dst, send_sem=send, recv_sem=recv, device_id=device, device_id_type=MESH
        )

    def place(b):
        if b == 0:
            return z, None
        if b < depth:
            return z - b, z >= b
        return z + (b - depth + 1), z + (b - depth + 1) < depth

    def guarded(cond, fn):
        if cond is None:
            fn()
        else:
            pl.when(cond)(fn)

    def both(a, b):
        return b if a is None else a if b is None else jnp.logical_and(a, b)

    def hops(b):
        moves = []
        if b < depth - 1:
            moves.append((b + 1, up, has_up, b))
        if b == 0 or depth <= b < 2 * depth - 2:
            landing = depth if b == 0 else b + 1
            moves.append((landing, down, has_down, depth - 1 + (landing - depth)))
        return moves

    def az(b, move, q):
        landing, device, unused, sem = move
        src = bufs[b][q].at[x, first_cols]
        return copy(src, bufs[landing][q].at[x, first_cols], az_send.at[sem, q], az_recv.at[landing, q], device)

    def bz(b, move, q):
        landing, device, unused, sem = move
        return copy(bufs[b][q].at[:, second_cols], bufs[landing][q].at[:, second_cols], bz_send.at[sem, q], bz_recv.at[landing, q], device)

    def ax(b, q):
        src = bufs[b][q].at[x, first_cols]
        return copy(src, src, ax_send.at[b, q], ax_recv.at[b, q], across)

    def az_wait(b, q):
        dst = bufs[b][q].at[x, first_cols]
        copy(dst, dst, az_send.at[0, q], az_recv.at[b, q], up).wait_recv()

    def bz_wait(b):
        for q in range(PIECES):
            dst = bufs[b][q].at[:, second_cols]
            copy(dst, dst, bz_send.at[0, q], bz_recv.at[b, q], up).wait_recv()

    def ax_wait(b, qs):
        for q in qs:
            dst = bufs[b][q].at[1 - x, first_cols]
            copy(dst, dst, ax_send.at[b, q], ax_recv.at[b, q], across).wait_recv()

    own_v = pltpu.make_async_copy(v, v_own, local_sem.at[1])
    own_m = pltpu.make_async_copy(meta_v, meta, local_sem.at[3])

    def lay(r, carry):
        at = pl.ds(pl.multiple_of(r * size, size), size)
        for q in range(PIECES):
            pltpu.make_async_copy(t.at[pl.ds(q * chunk, chunk), at], bufs[0][q].at[x, r], lay_sem.at[q]).start()
        return carry

    lax.fori_loop(0, row_blocks, lay, 0, unroll=8)
    own_v.start()
    own_m.start()
    barrier = pltpu.get_barrier_semaphore()
    for device in (across, beside, twin):
        pl.semaphore_signal(barrier, inc=1, device_id=device, device_id_type=MESH)
    pl.when(has_up)(lambda: pl.semaphore_signal(barrier, inc=1, device_id=up, device_id_type=MESH))
    pl.when(has_down)(lambda: pl.semaphore_signal(barrier, inc=1, device_id=down, device_id_type=MESH))
    pl.semaphore_wait(barrier, 3 + has_up.astype(jnp.int32) + has_down.astype(jnp.int32))

    bxs = [copy(bufs[0][q].at[x, second_cols], bufs[0][q].at[x, second_cols], bx_send.at[q], bx_recv.at[q], across)
           for q in range(PIECES)]
    vy = copy(v, v_other, one_send.at[1], one_recv.at[1], beside)
    my = copy(meta_v, meta_in, one_send.at[2], one_recv.at[2], beside)
    for q in range(PIECES):
        pltpu.make_async_copy(bufs[0][q].at[x], bufs[0][q].at[x], lay_sem.at[q]).wait()
    for bx in bxs:
        bx.start()
    for q in range(PIECES):
        for move in hops(0):
            guarded(move[2], lambda move=move, q=q: az(0, move, q).start())
        ax(0, q).start()
    my.start()
    vy.start()
    for bx in bxs:
        bx.wait_recv()

    def second_own(k):
        for move, turn in zip(hops(0), (z, depth - 1 - z)):
            guarded(both(move[2], turn == k), lambda move=move: [bz(0, move, q).start() for q in range(PIECES)] and None)

    def forward(b, q):
        def run():
            az_wait(b, q)
            for move in hops(b):
                guarded(move[2], lambda move=move: az(b, move, q).start())
            ax(b, q).start()

        guarded(place(b)[1], run)

    def forward_second(b):
        def run():
            bz_wait(b)
            for move in hops(b):
                guarded(move[2], lambda move=move: [bz(b, move, q).start() for q in range(PIECES)] and None)

        guarded(place(b)[1], run)

    def steps(b):
        if b in (depth - 1, 2 * depth - 2):
            return [(pl.ds(q * chunk, chunk), chunk, (q,)) for q in range(PIECES)]
        return [(pl.ds(0, rows), rows, tuple(range(PIECES)))]

    def products(b, strip, stored, info, span, count, qs):
        zp = place(b)[0]

        def slot(s, carry):
            at_row = info[1, s]
            left = jnp.concatenate([bufs[b][q][side, at_row] for side in (0, 1) for q in qs], axis=0)
            new = jnp.dot(left, stored[info[0, s]], preferred_element_type=jnp.float32)
            runs[s + 1, : 2 * count] = new + runs[s, : 2 * count] * info[2, s].astype(jnp.float32)
            return carry

        runs[0] = jnp.zeros((2 * rows, size), jnp.float32)
        lax.fori_loop(0, slots, slot, 0, unroll=8)
        for c in range(col_blocks):
            value = runs[info[3, c] + 1, : 2 * count] * info[4, c].astype(jnp.float32)
            part[zp, strip, :, span, c * size:(c + 1) * size] = value.reshape(2, count, size)

    def core_copy(b, strip, i):
        zp, span = place(b)[0], steps(b)[i][0]
        return copy(part.at[zp, strip, :, span], core_in.at[zp % half, strip, :, span],
                    core_send.at[b, strip, i], core_recv.at[b, strip, i], twin)

    def target(b, i):
        return out.at[place(b)[0] % half * 2 + y, :, steps(b)[i][0]]

    def y_copy(b, i):
        return copy(y_out.at[place(b)[0] % half, :, steps(b)[i][0]], target(b, i), y_send.at[b, i], y_recv.at[b, i], beside)

    def own_copy(b, i):
        zp, span = place(b)[0], steps(b)[i][0]
        return pltpu.make_async_copy(own_out.at[zp % half, :, span], target(b, i), own_sem.at[b, i])

    def mine(b):
        return place(b)[0] // half == core

    def compute(b, i):
        span, count, qs = steps(b)[i]

        def run():
            ax_wait(b, qs)
            for strip, stored, info in ((0, v_other, meta_other), (1, v_own, meta)):
                products(b, strip, stored, info, span, count, qs)
                pl.when(jnp.logical_not(mine(b)))(lambda strip=strip: core_copy(b, strip, i).start())

        guarded(place(b)[1], run)

    def finish(b, i):
        def run():
            zp, span = place(b)[0], steps(b)[i][0]
            slot = zp % half
            core_copy(b, 0, i).wait_recv()
            y_out[slot, :, span] = part[zp, 0, :, span] + core_in[slot, 0, :, span]
            y_copy(b, i).start()
            core_copy(b, 1, i).wait_recv()
            own_out[slot, :, span] = part[zp, 1, :, span] + core_in[slot, 1, :, span]
            own_copy(b, i).start()

        guarded(both(place(b)[1], mine(b)), run)

    def at(k):
        return [0] if k == 0 else [k, depth - 1 + k]

    second_own(0)
    for k in range(1, depth):
        for q in range(PIECES):
            for b in at(k):
                forward(b, q)
        second_own(k)
    own_v.wait()
    own_m.wait()
    my.wait_recv()
    into = pltpu.make_async_copy(meta_in, meta_other, local_sem.at[2])
    into.start()
    into.wait()
    vy.wait_recv()
    waiting = [(0, 0)]
    compute(0, 0)
    for k in range(1, depth):
        for b in at(k):
            forward_second(b)
        for i in range(len(steps(k))):
            for todo in waiting:
                finish(*todo)
            waiting = [(b, i) for b in at(k)]
            for todo in waiting:
                compute(*todo)
    for todo in waiting:
        finish(*todo)

    for bx in bxs:
        bx.wait_send()
    vy.wait_send()
    my.wait_send()
    for b in range(2 * depth - 1):
        valid = place(b)[1]
        for move in hops(b):
            guarded(both(valid, move[2]), lambda b=b, move=move: [(az(b, move, q).wait_send(), bz(b, move, q).wait_send()) for q in range(PIECES)] and None)
        guarded(valid, lambda b=b: [ax(b, q).wait_send() for q in range(PIECES)] and None)
        other = jnp.logical_not(mine(b))
        for i in range(len(steps(b))):
            guarded(both(valid, other), lambda b=b, i=i: [core_copy(b, j, i).wait_send() for j in (0, 1)] and None)
            guarded(both(valid, mine(b)), lambda b=b, i=i: [y_copy(b, i).wait(), own_copy(b, i).wait()] and None)


def slot_table(places, count, col_blocks):
    total = places.shape[0]
    ids = jnp.arange(total, dtype=jnp.int32)
    cols = jnp.where(ids < count, places % col_blocks, col_blocks)
    key = cols * total + ids
    rank = jnp.sum((key[None, :] < key[:, None]).astype(jnp.int32), axis=1)
    hit = (rank[:, None] == ids[None, :]).astype(jnp.int32)
    order = jnp.sum(hit * ids[:, None], axis=0)
    row = jnp.sum(hit * (places // col_blocks)[:, None], axis=0)
    col = jnp.sum(hit * cols[:, None], axis=0)
    before = jnp.sum((rank[:, None] + 1 == ids[None, :]).astype(jnp.int32) * (cols + 1)[:, None], axis=0) - 1
    same = (col == before).astype(jnp.int32)
    each = jnp.arange(col_blocks, dtype=jnp.int32)
    last = jnp.sum((cols[None, :] <= each[:, None]).astype(jnp.int32), axis=1) - 1
    some = jnp.sum((cols[None, :] == each[:, None]).astype(jnp.int32), axis=1)
    lanes = -(-max(total, col_blocks) // 128) * 128

    def wide(a):
        return jnp.pad(a, (0, lanes - a.shape[0]))

    zero = jnp.zeros((lanes,), jnp.int32)
    return jnp.stack([wide(order), wide(row), wide(same), wide(jnp.maximum(last, 0)), wide(jnp.minimum(some, 1)), zero, zero, zero])


def ring_shards(width, wide_size, t_amps, v_blocks, block_pos, block_count):
    rows, columns = t_amps.shape
    slots, size = v_blocks.shape[2], v_blocks.shape[3]
    depth = wide_size // 4
    half, buffers = depth // 2, 2 * depth - 1
    strip = width // wide_size
    meta = slot_table(block_pos[0, 0], block_count[0, 0], strip // size)
    bf16, f32, i32 = jnp.bfloat16, jnp.float32, jnp.int32
    dma = pltpu.SemaphoreType.DMA
    out = pl.pallas_call(
        functools.partial(ladder_kernel, depth),
        out_shape=jax.ShapeDtypeStruct((half * 2, 2, rows, strip), f32),
        in_specs=[
            pl.BlockSpec(memory_space=pl.ANY),
            pl.BlockSpec(memory_space=pl.ANY),
            pl.BlockSpec(memory_space=pltpu.VMEM),
        ],
        out_specs=pl.BlockSpec(memory_space=pl.ANY),
        scratch_shapes=[pltpu.VMEM((2, columns // size, rows // PIECES, size), bf16)] * (buffers * PIECES) + [
            pltpu.VMEM((slots, size, size), bf16),
            pltpu.VMEM((slots, size, size), bf16),
            pltpu.VMEM(meta.shape, i32),
            pltpu.SMEM(meta.shape, i32),
            pltpu.SMEM(meta.shape, i32),
            pltpu.VMEM((slots + 1, 2 * rows, size), f32),
            pltpu.VMEM((depth, 2, 2, rows, strip), f32),
            pltpu.VMEM((half, 2, 2, rows, strip), f32),
            pltpu.VMEM((half, 2, rows, strip), f32),
            pltpu.VMEM((half, 2, rows, strip), f32),
            dma((buffers, PIECES)),
            dma((PIECES,)), dma((PIECES,)), dma((PIECES,)),
            dma((4,)),
            dma((2 * depth, PIECES)), dma((buffers, PIECES)),
            dma((2 * depth, PIECES)), dma((buffers, PIECES)),
            dma((buffers, PIECES)), dma((buffers, PIECES)),
            dma((3,)), dma((3,)),
            dma((buffers, 2, PIECES)), dma((buffers, 2, PIECES)),
            dma((buffers, PIECES)), dma((buffers, PIECES)),
        ],
        compiler_params=pltpu.CompilerParams(
            collective_id=0, has_side_effects=True, vmem_limit_bytes=36 * 1024 * 1024
        ),
    )(t_amps, v_blocks, meta)
    return out.reshape(half * 4 * rows, strip)


def solution(mesh):
    in_specs = (
        P("wide", "narrow"),
        P("narrow", "wide", None, None, None),
        P("narrow", "wide", None),
        P("narrow", "wide"),
    )
    out_specs = P("narrow", "wide")
    wide_size, narrow_size = mesh.shape["wide"], mesh.shape["narrow"]

    def program(t_amps, v_blocks, block_pos, block_count):
        width = t_amps.shape[1]
        if narrow_size == 2 and wide_size % 8 == 0:
            body = functools.partial(ring_shards, width, wide_size)
        else:
            body = functools.partial(dense_shards, width)
        run = jax.shard_map(body, mesh=mesh, in_specs=in_specs, out_specs=out_specs, check_vma=False)
        return run(t_amps, v_blocks, block_pos, block_count)

    return program
```

```python
import functools

import jax
import jax.numpy as jnp
from jax import lax
from jax.experimental import pallas as pl
from jax.experimental.pallas import tpu as pltpu
from jax.sharding import PartitionSpec as P

MESH = pl.DeviceIdType.MESH
PIECES = 2


def dense_shards(width, t_amps, v_blocks, block_pos, block_count):
    stored = v_blocks[0, 0]
    places = block_pos[0, 0]
    slot_count = block_count[0, 0]
    block_size = stored.shape[1]
    slot_total = stored.shape[0]
    row_blocks = t_amps.shape[1] // block_size
    col_blocks = width // (lax.axis_size("wide") * block_size)
    live_mask = (jnp.arange(slot_total, dtype=jnp.int32) < slot_count).astype(jnp.bfloat16)
    masked = stored * live_mask[:, None, None]
    dense_tile = jnp.zeros((row_blocks * col_blocks, block_size, block_size), jnp.bfloat16)
    dense_tile = dense_tile.at[places].add(masked)
    dense_tile = dense_tile.reshape(row_blocks, col_blocks, block_size, block_size)
    dense_tile = jnp.transpose(dense_tile, (0, 2, 1, 3)).reshape(row_blocks * block_size, col_blocks * block_size)
    gathered = lax.all_gather(t_amps, "wide", axis=0, tiled=True)
    partial_sum = jnp.dot(gathered, dense_tile, preferred_element_type=jnp.float32)
    return lax.psum_scatter(partial_sum, "narrow", scatter_dimension=0, tiled=True)


def ladder_kernel(depth, t, v_tile, meta_v, out, *scratch):
    held = scratch[: (2 * depth - 1) * PIECES]
    bufs = [held[b * PIECES:(b + 1) * PIECES] for b in range(2 * depth - 1)]
    (v_own, v_other, meta_in, meta, meta_other, runs, part, core_in, y_out, own_out, own_sem, lay_sem, bx_send, bx_recv, local_sem, az_send, az_recv, bz_send, bz_recv,
     ax_send, ax_recv, one_send, one_recv, core_send, core_recv, y_send, y_recv) = scratch[(2 * depth - 1) * PIECES:]
    wide, core = lax.axis_index("wide"), lax.axis_index("narrow")
    z, y, x = wide // 4, (wide // 2) % 2, wide % 2
    up, down = (wide + 4, core), (wide - 4, core)
    across = (wide + 1 - 2 * x, core)
    beside = (wide + 2 - 4 * y, core)
    twin = (wide, 1 - core)
    half = depth // 2
    pieces, row_blocks, chunk, unused = t.shape
    rows = pieces * chunk
    v = v_tile.at[0, 0]
    slots, size = v.shape[0], v.shape[1]
    col_blocks = out.shape[-1] // size
    second = row_blocks * 5 // 32
    first = row_blocks - second
    first_cols = pl.ds(0, first)
    second_cols = pl.ds(first, second)
    has_up, has_down = z < depth - 1, z > 0

    def copy(src, dst, send, recv, device):
        return pltpu.make_async_remote_copy(
            src_ref=src, dst_ref=dst, send_sem=send, recv_sem=recv, device_id=device, device_id_type=MESH
        )

    def place(b):
        if b == 0:
            return z, None
        if b < depth:
            return z - b, z >= b
        return z + (b - depth + 1), z + (b - depth + 1) < depth

    def guarded(cond, fn):
        if cond is None:
            fn()
        else:
            pl.when(cond)(fn)

    def both(a, b):
        return b if a is None else a if b is None else jnp.logical_and(a, b)

    def hops(b):
        moves = []
        if b < depth - 1:
            moves.append((b + 1, up, has_up, b))
        if b == 0 or depth <= b < 2 * depth - 2:
            landing = depth if b == 0 else b + 1
            moves.append((landing, down, has_down, depth - 1 + (landing - depth)))
        return moves

    def az(b, move, q):
        landing, device, unused, sem = move
        src = t.at[q, first_cols] if b == 0 else bufs[b][q].at[x, first_cols]
        return copy(src, bufs[landing][q].at[x, first_cols], az_send.at[sem, q], az_recv.at[landing, q], device)

    def bz(b, move, q):
        landing, device, unused, sem = move
        return copy(bufs[b][q].at[:, second_cols], bufs[landing][q].at[:, second_cols], bz_send.at[sem, q], bz_recv.at[landing, q], device)

    def ax(b, q):
        src = t.at[q, first_cols] if b == 0 else bufs[b][q].at[x, first_cols]
        return copy(src, bufs[b][q].at[x, first_cols], ax_send.at[b, q], ax_recv.at[b, q], across)

    def az_wait(b, q):
        dst = bufs[b][q].at[x, first_cols]
        copy(dst, dst, az_send.at[0, q], az_recv.at[b, q], up).wait_recv()

    def bz_wait(b):
        for q in range(PIECES):
            dst = bufs[b][q].at[:, second_cols]
            copy(dst, dst, bz_send.at[0, q], bz_recv.at[b, q], up).wait_recv()

    def ax_wait(b, qs):
        for q in qs:
            dst = bufs[b][q].at[1 - x, first_cols]
            copy(dst, dst, ax_send.at[b, q], ax_recv.at[b, q], across).wait_recv()

    own_v = pltpu.make_async_copy(v, v_own, local_sem.at[1])
    own_m = pltpu.make_async_copy(meta_v, meta, local_sem.at[3])

    lays = [pltpu.make_async_copy(t.at[q], bufs[0][q].at[x], lay_sem.at[q]) for q in range(PIECES)]
    for lay in lays:
        lay.start()
    own_v.start()
    own_m.start()
    barrier = pltpu.get_barrier_semaphore()
    for device in (across, beside, twin):
        pl.semaphore_signal(barrier, inc=1, device_id=device, device_id_type=MESH)
    pl.when(has_up)(lambda: pl.semaphore_signal(barrier, inc=1, device_id=up, device_id_type=MESH))
    pl.when(has_down)(lambda: pl.semaphore_signal(barrier, inc=1, device_id=down, device_id_type=MESH))
    pl.semaphore_wait(barrier, 3 + has_up.astype(jnp.int32) + has_down.astype(jnp.int32))

    bxs = [copy(t.at[q, second_cols], bufs[0][q].at[x, second_cols], bx_send.at[q], bx_recv.at[q], across)
           for q in range(PIECES)]
    vy = copy(v, v_other, one_send.at[1], one_recv.at[1], beside)
    my = copy(meta_v, meta_in, one_send.at[2], one_recv.at[2], beside)
    for q in range(PIECES):
        bxs[q].start()
        for move in hops(0):
            guarded(move[2], lambda move=move, q=q: az(0, move, q).start())
        ax(0, q).start()
    my.start()
    vy.start()
    for lay in lays:
        lay.wait()
    for bx in bxs:
        bx.wait_recv()

    def second_own(k):
        for move, turn in zip(hops(0), (z, depth - 1 - z)):
            guarded(both(move[2], turn == k), lambda move=move: [bz(0, move, q).start() for q in range(PIECES)] and None)

    def forward(b, q):
        def run():
            az_wait(b, q)
            for move in hops(b):
                guarded(move[2], lambda move=move: az(b, move, q).start())
            ax(b, q).start()

        guarded(place(b)[1], run)

    def forward_second(b):
        def run():
            bz_wait(b)
            for move in hops(b):
                guarded(move[2], lambda move=move: [bz(b, move, q).start() for q in range(PIECES)] and None)

        guarded(place(b)[1], run)

    def steps(b):
        if b in (depth - 1, 2 * depth - 2):
            return [(pl.ds(q * chunk, chunk), chunk, (q,)) for q in range(PIECES)]
        return [(pl.ds(0, rows), rows, tuple(range(PIECES)))]

    def products(b, strip, stored, info, span, count, qs):
        zp = place(b)[0]

        def slot(s, carry):
            at_row = info[1, s]
            left = jnp.concatenate([bufs[b][q][side, at_row] for side in (0, 1) for q in qs], axis=0)
            new = jnp.dot(left, stored[info[0, s]], preferred_element_type=jnp.float32)
            runs[s + 1, : 2 * count] = new + runs[s, : 2 * count] * info[2, s].astype(jnp.float32)
            return carry

        runs[0] = jnp.zeros((2 * rows, size), jnp.float32)
        lax.fori_loop(0, slots, slot, 0, unroll=8)
        for c in range(col_blocks):
            value = runs[info[3, c] + 1, : 2 * count] * info[4, c].astype(jnp.float32)
            part[zp, strip, :, span, c * size:(c + 1) * size] = value.reshape(2, count, size)

    def core_copy(b, strip, i):
        zp, span = place(b)[0], steps(b)[i][0]
        return copy(part.at[zp, strip, :, span], core_in.at[zp % half, strip, :, span],
                    core_send.at[b, strip, i], core_recv.at[b, strip, i], twin)

    def target(b, i):
        return out.at[place(b)[0] % half * 2 + y, :, steps(b)[i][0]]

    def y_copy(b, i):
        return copy(y_out.at[place(b)[0] % half, :, steps(b)[i][0]], target(b, i), y_send.at[b, i], y_recv.at[b, i], beside)

    def own_copy(b, i):
        zp, span = place(b)[0], steps(b)[i][0]
        return pltpu.make_async_copy(own_out.at[zp % half, :, span], target(b, i), own_sem.at[b, i])

    def mine(b):
        return place(b)[0] // half == core

    def compute(b, i):
        span, count, qs = steps(b)[i]

        def run():
            ax_wait(b, qs)
            for strip, stored, info in ((0, v_other, meta_other), (1, v_own, meta)):
                products(b, strip, stored, info, span, count, qs)
                pl.when(jnp.logical_not(mine(b)))(lambda strip=strip: core_copy(b, strip, i).start())

        guarded(place(b)[1], run)

    def finish(b, i):
        def run():
            zp, span = place(b)[0], steps(b)[i][0]
            slot = zp % half
            core_copy(b, 0, i).wait_recv()
            y_out[slot, :, span] = part[zp, 0, :, span] + core_in[slot, 0, :, span]
            y_copy(b, i).start()
            core_copy(b, 1, i).wait_recv()
            own_out[slot, :, span] = part[zp, 1, :, span] + core_in[slot, 1, :, span]
            own_copy(b, i).start()

        guarded(both(place(b)[1], mine(b)), run)

    def at(k):
        return [0] if k == 0 else [k, depth - 1 + k]

    second_own(0)
    for k in range(1, depth):
        for q in range(PIECES):
            for b in at(k):
                forward(b, q)
        second_own(k)
    own_v.wait()
    own_m.wait()
    my.wait_recv()
    into = pltpu.make_async_copy(meta_in, meta_other, local_sem.at[2])
    into.start()
    into.wait()
    vy.wait_recv()
    waiting = [(0, 0)]
    compute(0, 0)
    for k in range(1, depth):
        for b in at(k):
            forward_second(b)
        for i in range(len(steps(k))):
            for todo in waiting:
                finish(*todo)
            waiting = [(b, i) for b in at(k)]
            for todo in waiting:
                compute(*todo)
    for todo in waiting:
        finish(*todo)

    for bx in bxs:
        bx.wait_send()
    vy.wait_send()
    my.wait_send()
    for b in range(2 * depth - 1):
        valid = place(b)[1]
        for move in hops(b):
            guarded(both(valid, move[2]), lambda b=b, move=move: [(az(b, move, q).wait_send(), bz(b, move, q).wait_send()) for q in range(PIECES)] and None)
        guarded(valid, lambda b=b: [ax(b, q).wait_send() for q in range(PIECES)] and None)
        other = jnp.logical_not(mine(b))
        for i in range(len(steps(b))):
            guarded(both(valid, other), lambda b=b, i=i: [core_copy(b, j, i).wait_send() for j in (0, 1)] and None)
            guarded(both(valid, mine(b)), lambda b=b, i=i: [y_copy(b, i).wait(), own_copy(b, i).wait()] and None)


def slot_table(places, count, col_blocks):
    total = places.shape[0]
    ids = jnp.arange(total, dtype=jnp.int32)
    cols = jnp.where(ids < count, places % col_blocks, col_blocks)
    key = cols * total + ids
    rank = jnp.sum((key[None, :] < key[:, None]).astype(jnp.int32), axis=1)
    hit = (rank[:, None] == ids[None, :]).astype(jnp.int32)
    order = jnp.sum(hit * ids[:, None], axis=0)
    row = jnp.sum(hit * (places // col_blocks)[:, None], axis=0)
    col = jnp.sum(hit * cols[:, None], axis=0)
    before = jnp.sum((rank[:, None] + 1 == ids[None, :]).astype(jnp.int32) * (cols + 1)[:, None], axis=0) - 1
    same = (col == before).astype(jnp.int32)
    each = jnp.arange(col_blocks, dtype=jnp.int32)
    last = jnp.sum((cols[None, :] <= each[:, None]).astype(jnp.int32), axis=1) - 1
    some = jnp.sum((cols[None, :] == each[:, None]).astype(jnp.int32), axis=1)
    lanes = -(-max(total, col_blocks) // 128) * 128

    def wide(a):
        return jnp.pad(a, (0, lanes - a.shape[0]))

    zero = jnp.zeros((lanes,), jnp.int32)
    return jnp.stack([wide(order), wide(row), wide(same), wide(jnp.maximum(last, 0)), wide(jnp.minimum(some, 1)), zero, zero, zero])


def ring_shards(width, wide_size, t_amps, v_blocks, block_pos, block_count):
    rows, columns = t_amps.shape
    slots, size = v_blocks.shape[2], v_blocks.shape[3]
    depth = wide_size // 4
    half, buffers = depth // 2, 2 * depth - 1
    strip = width // wide_size
    meta = slot_table(block_pos[0, 0], block_count[0, 0], strip // size)
    by_piece = jnp.transpose(t_amps.reshape(PIECES, rows // PIECES, columns // size, size), (0, 2, 1, 3))
    bf16, f32, i32 = jnp.bfloat16, jnp.float32, jnp.int32
    dma = pltpu.SemaphoreType.DMA
    out = pl.pallas_call(
        functools.partial(ladder_kernel, depth),
        out_shape=jax.ShapeDtypeStruct((half * 2, 2, rows, strip), f32),
        in_specs=[
            pl.BlockSpec(memory_space=pl.ANY),
            pl.BlockSpec(memory_space=pl.ANY),
            pl.BlockSpec(memory_space=pltpu.VMEM),
        ],
        out_specs=pl.BlockSpec(memory_space=pl.ANY),
        scratch_shapes=[pltpu.VMEM((2, columns // size, rows // PIECES, size), bf16)] * (buffers * PIECES) + [
            pltpu.VMEM((slots, size, size), bf16),
            pltpu.VMEM((slots, size, size), bf16),
            pltpu.VMEM(meta.shape, i32),
            pltpu.SMEM(meta.shape, i32),
            pltpu.SMEM(meta.shape, i32),
            pltpu.VMEM((slots + 1, 2 * rows, size), f32),
            pltpu.VMEM((depth, 2, 2, rows, strip), f32),
            pltpu.VMEM((half, 2, 2, rows, strip), f32),
            pltpu.VMEM((half, 2, rows, strip), f32),
            pltpu.VMEM((half, 2, rows, strip), f32),
            dma((buffers, PIECES)),
            dma((PIECES,)), dma((PIECES,)), dma((PIECES,)),
            dma((4,)),
            dma((2 * depth, PIECES)), dma((buffers, PIECES)),
            dma((2 * depth, PIECES)), dma((buffers, PIECES)),
            dma((buffers, PIECES)), dma((buffers, PIECES)),
            dma((3,)), dma((3,)),
            dma((buffers, 2, PIECES)), dma((buffers, 2, PIECES)),
            dma((buffers, PIECES)), dma((buffers, PIECES)),
        ],
        compiler_params=pltpu.CompilerParams(
            collective_id=0, has_side_effects=True, vmem_limit_bytes=36 * 1024 * 1024
        ),
    )(by_piece, v_blocks, meta)
    return out.reshape(half * 4 * rows, strip)


def solution(mesh):
    in_specs = (
        P("wide", "narrow"),
        P("narrow", "wide", None, None, None),
        P("narrow", "wide", None),
        P("narrow", "wide"),
    )
    out_specs = P("narrow", "wide")
    wide_size, narrow_size = mesh.shape["wide"], mesh.shape["narrow"]

    def program(t_amps, v_blocks, block_pos, block_count):
        width = t_amps.shape[1]
        if narrow_size == 2 and wide_size % 8 == 0:
            body = functools.partial(ring_shards, width, wide_size)
        else:
            body = functools.partial(dense_shards, width)
        run = jax.shard_map(body, mesh=mesh, in_specs=in_specs, out_specs=out_specs, check_vma=False)
        return run(t_amps, v_blocks, block_pos, block_count)

    return program
```
